512 devices in a mesh: section: 2 (over core), tm: 32 (over x, z), tile: 8 (over y).
Axes of the slice: x: 4, y: 8, z: 8, core: 2. Of those that a mesh axis runs over, the one named last changes fastest.
Arguments:
- features: bfloat16 [64, 64, 64, 256], P('tm', 'tile', None, 'section'), may hold values from -320 to 320
- norm_gain_in: float32 [256], replicated, may hold values from 0.1 to 1.9
- norm_shift_in: float32 [256], replicated, may hold values from -0.8 to 0.8
- conv_in_weight: bfloat16 [3, 3, 3, 256, 128], replicated, may hold values from -0.078125 to 0.078125
- conv_in_bias: float32 [128], replicated, may hold values from -1 to 1
- norm_gain_mid: float32 [128], replicated, may hold values from 0.1 to 1.9
- norm_shift_mid: float32 [128], replicated, may hold values from -0.8 to 0.8
- conv_mid_weight: bfloat16 [3, 3, 3, 128, 128], replicated, may hold values from -0.109375 to 0.109375
- conv_mid_bias: float32 [128], replicated, may hold values from -0.6 to 0.6
- skip_weight: bfloat16 [256, 128], replicated, may hold values from -0.09375 to 0.09375
- skip_bias: float32 [128], replicated, may hold values from -0.6 to 0.6
Outputs:
- block_out: bfloat16 [64, 64, 64, 128], P('tm', 'tile', 'section')
The draws below stay inside these ranges and needn't reach their ends.
All inputs are finite; a program needn't handle non-finite values.
Results may differ from the reference program's by a relative error of at most 0.008.
Values may be sent and summed in bfloat16 or wider, within the bound.
A program may use at most 64 MiB of HBM per device.

```python
import jax
import jax.numpy as jnp
from jax import lax

CIN = 256
COUT = 128
GROUPS = 32
FR_DEV = 2
ROWS_DEV = 8
FRAMES = 64
ROWS = 64
COLS = 64


log_ten = 2.302585093


two_pi = 6.283185307


def amplitude_profile(key, count):
    key_slope, key_sign, key_phase, key_rough = jax.random.split(key, 4)
    position = jnp.arange(count, dtype=jnp.float32) / max(count - 1, 1)
    slope = jax.random.uniform(key_slope, (), jnp.float32, 0.3, 0.5)
    flip = (2 * jax.random.randint(key_sign, (), 0, 2) - 1).astype(jnp.float32)
    phase = jax.random.uniform(key_phase, (), jnp.float32, 0.0, 1.0)
    rough = jax.random.uniform(key_rough, (count,), jnp.float32, 0.0, 1.0)
    return flip * slope * (position - 0.5) + 0.12 * jnp.sin(two_pi * (1.5 * position + phase)) + 0.12 * rough


def draw_features(key, part):
    keys = jax.random.split(key, 8)
    shape = (FRAMES, ROWS, COLS, CIN)
    noise = jnp.clip(jax.random.normal(keys[0], shape, jnp.float32), -5.0, 5.0)
    offset = jax.random.uniform(keys[1], (CIN,), jnp.float32, -1.0, 1.0)
    time_offset = jax.random.uniform(keys[2], (FRAMES // FR_DEV, CIN), jnp.float32, -0.8, 0.8)
    tile_offset = jax.random.uniform(keys[3], (ROWS // ROWS_DEV, CIN), jnp.float32, -0.5, 0.5)
    time_offset = jnp.repeat(time_offset, FR_DEV, axis=0)
    tile_offset = jnp.repeat(tile_offset, ROWS_DEV, axis=0)
    frame_exp = amplitude_profile(keys[4], FRAMES)
    row_exp = amplitude_profile(keys[5], ROWS)
    col_pos = jnp.arange(COLS, dtype=jnp.float32) / max(COLS - 1, 1)
    rough = jax.random.uniform(keys[6], (FRAMES, ROWS, COLS, 1), jnp.float32)
    chan_pos = jax.random.uniform(keys[7], (CIN,), jnp.float32)
    exponent = frame_exp[:, None, None, None] + row_exp[None, :, None, None] + 0.5 * col_pos[None, None, :, None] + 0.25 * rough
    scale = jnp.exp(log_ten * exponent) * jnp.exp(log_ten * 0.1 * chan_pos)
    shifted = noise + offset + time_offset[:, None, None, :] + tile_offset[None, :, None, :]
    return (scale * shifted).astype(jnp.bfloat16)


def normal_values(rng, extent, scale, most, kind=jnp.bfloat16):
    return jnp.clip(scale * jax.random.normal(rng, extent, jnp.float32), -most, most).astype(kind)


def setup_inputs(seed: int = 0) -> dict:
    seeds = jax.random.split(jax.random.key(seed), 12)
    features = draw_features(jax.random.fold_in(seeds[11], 71), 0)
    norm_gain_in = jnp.clip(1.0 + 0.18 * jax.random.normal(seeds[1], (CIN,), jnp.float32), 0.1, 1.9)
    norm_shift_in = jnp.clip(jax.random.uniform(seeds[2], (CIN,), jnp.float32, -0.8, 0.8), -0.8, 0.8)
    conv_in_weight = normal_values(seeds[3], (3, 3, 3, CIN, COUT), (27 * CIN) ** -0.5, 0.078125)
    conv_in_bias = jnp.clip(jax.random.uniform(seeds[4], (COUT,), jnp.float32, -1.0, 1.0), -1.0, 1.0)
    norm_gain_mid = jnp.clip(1.0 + 0.18 * jax.random.normal(seeds[5], (COUT,), jnp.float32), 0.1, 1.9)
    norm_shift_mid = jnp.clip(jax.random.uniform(seeds[6], (COUT,), jnp.float32, -0.8, 0.8), -0.8, 0.8)
    conv_mid_weight = normal_values(seeds[7], (3, 3, 3, COUT, COUT), (27 * COUT) ** -0.5, 0.109375)
    conv_mid_bias = jnp.clip(jax.random.uniform(seeds[8], (COUT,), jnp.float32, -0.6, 0.6), -0.6, 0.6)
    skip_weight = normal_values(seeds[9], (CIN, COUT), (16 * CIN) ** -0.5, 0.09375)
    skip_bias = jnp.clip(jax.random.uniform(seeds[10], (COUT,), jnp.float32, -0.6, 0.6), -0.6, 0.6)
    return {"features": features, "norm_gain_in": norm_gain_in, "norm_shift_in": norm_shift_in, "conv_in_weight": conv_in_weight, "conv_in_bias": conv_in_bias, "norm_gain_mid": norm_gain_mid, "norm_shift_mid": norm_shift_mid, "conv_mid_weight": conv_mid_weight, "conv_mid_bias": conv_mid_bias, "skip_weight": skip_weight, "skip_bias": skip_bias}


def group_norm_act(values, norm_gain, norm_shift):
    frames, rows, columns, channels = values.shape
    grouped = values.reshape(frames, rows, columns, GROUPS, channels // GROUPS)
    group_mean = lax.optimization_barrier(jnp.mean(grouped, axis=(0, 1, 2, 4), keepdims=True))
    centered = grouped - group_mean
    spread = lax.optimization_barrier(jnp.mean(centered * centered, axis=(0, 1, 2, 4), keepdims=True))
    normed = (centered * lax.rsqrt(spread + 1e-06)).reshape(values.shape)
    return jax.nn.silu(normed * norm_gain + norm_shift).astype(jnp.bfloat16)

def convolve(active, weights, conv_bias):
    padded = jnp.pad(active.astype(jnp.float32), ((2, 0), (1, 1), (1, 1), (0, 0)), mode='edge')
    summed = lax.conv_general_dilated(padded[None], weights.astype(jnp.float32), (1, 1, 1), 'VALID', dimension_numbers=('NDHWC', 'DHWIO', 'NDHWC'), precision=lax.Precision.HIGHEST)
    return summed[0] + conv_bias

def reference(features, norm_gain_in, norm_shift_in, conv_in_weight, conv_in_bias, norm_gain_mid, norm_shift_mid, conv_mid_weight, conv_mid_bias, skip_weight, skip_bias):
    act_in = group_norm_act(features.astype(jnp.float32), norm_gain_in, norm_shift_in)
    hidden = convolve(act_in, conv_in_weight, conv_in_bias).astype(jnp.bfloat16)
    act_mid = group_norm_act(hidden.astype(jnp.float32), norm_gain_mid, norm_shift_mid)
    residual = convolve(act_mid, conv_mid_weight, conv_mid_bias)
    shortcut = jnp.einsum('frck,ko->frco', features.astype(jnp.float32), skip_weight.astype(jnp.float32), precision=lax.Precision.HIGHEST) + skip_bias
    return (residual + shortcut).astype(jnp.bfloat16)
```

```python
import functools

import jax
import jax.numpy as jnp
from jax import lax
from jax.experimental import pallas as pl
from jax.experimental.pallas import tpu as pltpu
from jax.sharding import PartitionSpec as P

MESH = pl.DeviceIdType.MESH
EPS = 1e-06
F32 = jnp.float32
BF16 = jnp.bfloat16


def ring_distance(step, size):
    return min(step % size, (-step) % size)


def lane_group_sum(values, width):
    lanes = values.shape[-1]
    lane = lax.broadcasted_iota(jnp.int32, values.shape, values.ndim - 1)
    step = 1
    while step < width:
        upper = lax.rem(lane, 2 * step) >= step
        values = values + jnp.where(
            upper, pltpu.roll(values, step, 1), pltpu.roll(values, lanes - step, 1)
        )
        step *= 2
    return values


def combine(own, others, count):
    parts = others.shape[0] + 1
    total = own + jnp.sum(others, axis=0)
    mean = total * (1.0 / parts)
    spread = jnp.square(own - mean) + jnp.sum(jnp.square(others - mean[None]), axis=0)
    row = lax.broadcasted_iota(jnp.int32, own.shape, 0)
    return jnp.where(row == 0, mean, total + count * spread[0:1])


def silu(values):
    return values / (1.0 + jnp.exp(-values))


def kernel(
    sizes,
    features, gain_in, shift_in, w_in, b_in, gain_mid, shift_mid, w_mid, b_mid, w_skip, b_skip,
    out,
    x_ref, h_ref, act, w1, w2, ws, small,
    part_own, part_in, skip_own, skip_out, skip_in,
    stat_out, y_buf, xz_buf,
    load_sem, stat_send, stat_recv, halo_send, halo_recv, part_send, part_recv,
):
    nx, nz, ny = sizes
    s, tm, y = lax.axis_index("section"), lax.axis_index("tm"), lax.axis_index("tile")
    ntm = nx * nz
    x, z = tm // nz, lax.rem(tm, nz)
    frames, rows, cols, lanes = features.shape
    half = cols // 2
    wide = half + 16
    cells = frames * rows * cols

    def device(d_tm=None, d_y=0, plane=None, other=False):
        new_tm = tm
        if d_tm is not None:
            new_tm = lax.rem(tm + d_tm + ntm, ntm)
        if plane is not None:
            new_tm = lax.rem(x + plane[0], nx) * nz + lax.rem(z + plane[1], nz)
        new_y = lax.rem(y + d_y + ny, ny) if d_y else y
        return {"section": 1 - s if other else s, "tm": new_tm, "tile": new_y}

    y_steps = sorted(range(1, ny), key=lambda d: -ring_distance(d, ny))
    plane_steps = sorted(
        [(a, b) for a in range(nx) for b in range(nz) if (a, b) != (0, 0)],
        key=lambda d: -ring_distance(d[0], nx) - ring_distance(d[1], nz),
    )
    y_devices = [device(d_y=d) for d in y_steps]
    plane_devices = [device(plane=d) for d in plane_steps]
    partner = device(other=True)
    corner_devices = [device(d_tm=a, d_y=b) for a in (1, -1) for b in (1, -1)]

    barrier = pltpu.get_barrier_semaphore()
    greeted = plane_devices + y_devices + corner_devices + [partner]
    for peer in greeted:
        pl.semaphore_signal(barrier, inc=1, device_id=peer, device_id_type=MESH)

    own_frames, own_rows = pl.ds(frames, frames), pl.ds(1, rows)
    lower = pl.multiple_of(s * lanes, lanes)
    loads = [
        pltpu.make_async_copy(features, x_ref.at[own_frames, own_rows], load_sem.at[0]),
        pltpu.make_async_copy(w_skip.at[pl.ds(lower, lanes)], ws, load_sem.at[1]),
        pltpu.make_async_copy(w_in.at[:, :, :, pl.ds(lower, lanes)], w1, load_sem.at[2]),
        pltpu.make_async_copy(w_mid, w2, load_sem.at[3]),
    ]
    vectors = [gain_in.at[pl.ds(lower, lanes)], shift_in.at[pl.ds(lower, lanes)], b_in, gain_mid, shift_mid, b_mid, b_skip]
    for i, vector in enumerate(vectors):
        loads.append(pltpu.make_async_copy(vector, small.at[i], load_sem.at[4 + i]))
    for load in loads:
        load.start()

    def local_stats(ref, width):
        def add(i, total):
            block = ref[frames + i // rows, 1 + lax.rem(i, rows)].astype(F32)
            return total + jnp.sum(block.reshape(cols // 8, 8, lanes), axis=0)

        total = lax.fori_loop(0, frames * rows, add, jnp.zeros((8, lanes), F32), unroll=4)
        total = jnp.sum(total, axis=0, keepdims=True)
        mean = lane_group_sum(jnp.broadcast_to(total, (8, lanes)), width) * (1.0 / (cells * width))

        def add_square(i, total):
            block = ref[frames + i // rows, 1 + lax.rem(i, rows)].astype(F32).reshape(cols // 8, 8, lanes)
            return total + jnp.sum(jnp.square(block - mean[None]), axis=0)

        spread = lax.fori_loop(0, frames * rows, add_square, jnp.zeros((8, lanes), F32), unroll=4)
        spread = jnp.sum(spread, axis=0, keepdims=True)
        spread = lane_group_sum(jnp.broadcast_to(spread, (8, lanes)), width)
        row = lax.broadcasted_iota(jnp.int32, (8, lanes), 0)
        return jnp.where(row == 0, mean, spread)

    def stat_phase(which, tile, devices, buffer):
        stat_out[which] = tile
        for j, peer in enumerate(devices):
            pltpu.make_async_remote_copy(
                src_ref=stat_out.at[which], dst_ref=buffer.at[which // 2, j],
                send_sem=stat_send.at[which], recv_sem=stat_recv.at[which],
                device_id=peer, device_id_type=MESH,
            ).start()

    def stat_wait(which, buffer):
        received = buffer.at[which // 2]
        pltpu.make_async_copy(received, received, stat_recv.at[which]).wait()
        return received[...]

    def stat_done(which, buffer):
        received = buffer.at[which // 2]
        pltpu.make_async_copy(received, received, stat_send.at[which]).wait()

    def halos(ref, at_cols, base):
        last = rows
        moves = [
            ((own_frames, own_rows), (pl.ds(0, frames), own_rows), device(d_tm=1)),
            ((own_frames, last), (own_frames, 0), device(d_y=1)),
            ((own_frames, 1), (own_frames, rows + 1), device(d_y=-1)),
            ((own_frames, last), (pl.ds(0, frames), 0), device(d_tm=1, d_y=1)),
            ((own_frames, 1), (pl.ds(0, frames), rows + 1), device(d_tm=1, d_y=-1)),
        ]
        return [
            pltpu.make_async_remote_copy(
                src_ref=ref.at[(*source, at_cols)], dst_ref=ref.at[(*target, at_cols)],
                send_sem=halo_send.at[base + i], recv_sem=halo_recv.at[base + i],
                device_id=peer, device_id_type=MESH,
            )
            for i, (source, target, peer) in enumerate(moves)
        ]

    def scales(tile, count, gain, shift):
        mean, spread = tile[0:1], tile[1:2] * (1.0 / count)
        scale = lax.rsqrt(spread + EPS) * small[gain:gain + 1, :]
        return mean, scale, small[shift:shift + 1, :]

    def activate(ref, at_cols, width, mean, scale, shift):
        place = lax.broadcasted_iota(jnp.int32, (width, lanes), 0)

        def one(i, carry):
            f, r = i // (rows + 2), lax.rem(i, rows + 2)
            from_f = jnp.where(tm == 0, jnp.maximum(f, frames), f)
            from_r = jnp.where(y == 0, jnp.maximum(r, 1), r)
            from_r = jnp.where(y == ny - 1, jnp.minimum(from_r, rows), from_r)
            block = ref[from_f, from_r, at_cols].astype(F32)
            block = silu((block - mean) * scale + shift)
            left = jnp.where(place == 0, block, pltpu.roll(block, 1, 0))
            right = jnp.where(place == width - 1, block, pltpu.roll(block, width - 1, 0))
            act[0, f, r, 0:width] = left.astype(BF16)
            act[1, f, r, 0:width] = block.astype(BF16)
            act[2, f, r, 0:width] = right.astype(BF16)
            return carry

        lax.fori_loop(0, 2 * frames * (rows + 2), one, 0, unroll=2)

    def convolve(weights, f, r, n_rows, at_cols, n_cols):
        taps = [(t, i, j) for t in range(3) for i in range(3) for j in range(3)]
        windows = [
            act[j, f + t, pl.ds(r + i, n_rows), at_cols].reshape(n_rows * n_cols, lanes) for t, i, j in taps
        ]
        total = jnp.zeros((n_rows * n_cols, lanes), F32)
        for k in range(0, len(taps), 2):
            window = jnp.concatenate(windows[k:k + 2], axis=1)
            matrix = jnp.concatenate([weights[tap] for tap in taps[k:k + 2]], axis=0)
            total = total + jnp.dot(window, matrix, preferred_element_type=F32)
        return total

    loads[0].wait()
    tile = local_stats(x_ref, 8)
    pl.semaphore_wait(barrier, len(greeted))
    stat_phase(0, tile, y_devices, y_buf)
    feature_halos = halos(x_ref, slice(None), 0)
    for copy in feature_halos:
        copy.start()

    loads[1].wait()
    their_cols, our_cols = pl.multiple_of((1 - s) * half, half), pl.multiple_of(s * half, half)

    def skip_product(start):
        block = x_ref[own_frames, own_rows, pl.ds(start, half)].reshape(frames * rows * half, lanes)
        return jnp.dot(block, ws[...], preferred_element_type=F32)

    skip_out[...] = skip_product(their_cols)
    skip_copy = pltpu.make_async_remote_copy(
        src_ref=skip_out, dst_ref=skip_in, send_sem=part_send.at[0], recv_sem=part_recv.at[0],
        device_id=partner, device_id_type=MESH,
    )
    skip_copy.start()
    skip_own[...] = skip_product(our_cols)
    for load in loads[2:]:
        load.wait()

    tile = combine(tile, stat_wait(0, y_buf), float(cells * 8))
    stat_phase(1, tile, plane_devices, xz_buf)
    tile = combine(tile, stat_wait(1, xz_buf), float(cells * 8 * ny))
    mean, scale, shift = scales(tile, float(cells * 8 * ny * ntm), 0, 1)
    for copy in feature_halos:
        copy.wait_recv()
    activate(x_ref, slice(None), cols, mean, scale, shift)

    pieces = part_own.shape[0]
    piece_rows = rows * frames // pieces
    part_copies = [
        pltpu.make_async_remote_copy(
            src_ref=part_own.at[i], dst_ref=part_in.at[i],
            send_sem=part_send.at[1 + i], recv_sem=part_recv.at[1 + i],
            device_id=partner, device_id_type=MESH,
        )
        for i in range(pieces)
    ]
    for i in range(pieces):
        f, r = (i * piece_rows) // rows, (i * piece_rows) % rows
        part_own[i] = convolve(w1, f, r, piece_rows, slice(None), cols)
        part_copies[i].start()
    for i in range(pieces):
        f, r = (i * piece_rows) // rows, (i * piece_rows) % rows
        part_copies[i].wait_recv()
        hidden = part_own[i] + part_in[i] + small[2:3, :]
        h_ref[frames + f, 1 + r:1 + r + piece_rows] = hidden.astype(BF16).reshape(piece_rows, cols, lanes)

    tile = local_stats(h_ref, 4)
    stat_phase(2, tile, y_devices, y_buf)
    wide_start = pl.multiple_of(s * 16, 16)
    wide_cols = pl.ds(wide_start, wide)
    hidden_halos = halos(h_ref, wide_cols, len(feature_halos))
    for copy in hidden_halos:
        copy.start()
    skip_copy.wait_recv()
    skip_own[...] = skip_own[...] + skip_in[...] + (small[5:6, :] + small[6:7, :])
    tile = combine(tile, stat_wait(2, y_buf), float(cells * 4))
    stat_phase(3, tile, plane_devices, xz_buf)
    tile = combine(tile, stat_wait(3, xz_buf), float(cells * 4 * ny))
    mean, scale, shift = scales(tile, float(cells * 4 * ny * ntm), 3, 4)
    for copy in hidden_halos:
        copy.wait_recv()
    activate(h_ref, wide_cols, wide, mean, scale, shift)

    for f in range(frames):
        size = rows * half
        total = convolve(w2, f, 0, rows, pl.ds(wide_start, half), half)
        total = total + skip_own[f * size:(f + 1) * size, :]
        out[f] = total.astype(BF16).reshape(rows, half, lanes)

    for copy in feature_halos + hidden_halos + part_copies + [skip_copy]:
        copy.wait_send()
    for which, buffer in ((0, y_buf), (1, xz_buf), (2, y_buf), (3, xz_buf)):
        stat_done(which, buffer)


def shards(sizes, features, *others):
    nx, nz, ny = sizes
    frames, rows, cols, lanes = features.shape
    cells = frames * rows * cols
    pieces = 4
    dma = pltpu.SemaphoreType.DMA
    return pl.pallas_call(
        functools.partial(kernel, sizes),
        out_shape=jax.ShapeDtypeStruct((frames, rows, cols // 2, lanes), BF16),
        in_specs=[pl.BlockSpec(memory_space=pl.ANY)] * 11,
        out_specs=pl.BlockSpec(memory_space=pltpu.VMEM),
        scratch_shapes=[
            pltpu.VMEM((2 * frames, rows + 2, cols, lanes), BF16),
            pltpu.VMEM((2 * frames, rows + 2, cols, lanes), BF16),
            pltpu.VMEM((3, 2 * frames, rows + 2, cols, lanes), BF16),
            pltpu.VMEM((3, 3, 3, lanes, lanes), BF16),
            pltpu.VMEM((3, 3, 3, lanes, lanes), BF16),
            pltpu.VMEM((lanes, lanes), BF16),
            pltpu.VMEM((7, lanes), F32),
            pltpu.VMEM((pieces, cells // pieces, lanes), F32),
            pltpu.VMEM((pieces, cells // pieces, lanes), F32),
            pltpu.VMEM((cells // 2, lanes), F32),
            pltpu.VMEM((cells // 2, lanes), F32),
            pltpu.VMEM((cells // 2, lanes), F32),
            pltpu.VMEM((4, 8, lanes), F32),
            pltpu.VMEM((2, ny - 1, 8, lanes), F32),
            pltpu.VMEM((2, nx * nz - 1, 8, lanes), F32),
            dma((11,)), dma((4,)), dma((4,)), dma((10,)), dma((10,)), dma((pieces + 1,)), dma((pieces + 1,)),
        ],
        compiler_params=pltpu.CompilerParams(
            collective_id=0, has_side_effects=True, vmem_limit_bytes=40 * 2**20
        ),
        name="residual_block",
    )(features, *others)


def solution(mesh):
    nz = 8 if mesh.shape["tm"] % 8 == 0 else 2
    sizes = (mesh.shape["tm"] // nz, nz, mesh.shape["tile"])
    in_specs = (P("tm", "tile", None, "section"), P(), P(), P(), P(), P(), P(), P(), P(), P(), P())
    return jax.shard_map(
        functools.partial(shards, sizes), mesh=mesh, in_specs=in_specs,
        out_specs=P("tm", "tile", "section", None), check_vma=False,
    )
```

```python
import functools

import jax
import jax.numpy as jnp
from jax import lax
from jax.experimental import pallas as pl
from jax.experimental.pallas import tpu as pltpu
from jax.sharding import PartitionSpec as P

MESH = pl.DeviceIdType.MESH
EPS = 1e-06
F32 = jnp.float32
BF16 = jnp.bfloat16


def ring_distance(step, size):
    return min(step % size, (-step) % size)


def lane_group_sum(values, width):
    lanes = values.shape[-1]
    lane = lax.broadcasted_iota(jnp.int32, values.shape, values.ndim - 1)
    step = 1
    while step < width:
        upper = lax.rem(lane, 2 * step) >= step
        values = values + jnp.where(
            upper, pltpu.roll(values, step, 1), pltpu.roll(values, lanes - step, 1)
        )
        step *= 2
    return values


def combine(own, others, count):
    parts = others.shape[0] + 1
    total = own + jnp.sum(others, axis=0)
    mean = total * (1.0 / parts)
    spread = jnp.square(own - mean) + jnp.sum(jnp.square(others - mean[None]), axis=0)
    row = lax.broadcasted_iota(jnp.int32, own.shape, 0)
    return jnp.where(row == 0, mean, total + count * spread[0:1])


def silu(values):
    return values / (1.0 + jnp.exp(-values))


def kernel(
    sizes,
    features, gain_in, shift_in, w_in, b_in, gain_mid, shift_mid, w_mid, b_mid, w_skip, b_skip,
    out,
    x_ref, h_ref, act, w1, w2, ws, small,
    part_own, part_in, skip_own, skip_out, skip_in,
    stat_out, y_buf, xz_buf,
    load_sem, stat_send, stat_recv, halo_send, halo_recv, part_send, part_recv,
):
    nx, nz, ny = sizes
    s, tm, y = lax.axis_index("section"), lax.axis_index("tm"), lax.axis_index("tile")
    ntm = nx * nz
    x, z = tm // nz, lax.rem(tm, nz)
    frames, rows, cols, lanes = features.shape
    half = cols // 2
    wide = half + 16
    cells = frames * rows * cols

    def device(d_tm=None, d_y=0, plane=None, other=False):
        new_tm = tm
        if d_tm is not None:
            new_tm = lax.rem(tm + d_tm + ntm, ntm)
        if plane is not None:
            new_tm = lax.rem(x + plane[0], nx) * nz + lax.rem(z + plane[1], nz)
        new_y = lax.rem(y + d_y + ny, ny) if d_y else y
        return {"section": 1 - s if other else s, "tm": new_tm, "tile": new_y}

    y_steps = sorted(range(1, ny), key=lambda d: -ring_distance(d, ny))
    plane_steps = sorted(
        [(a, b) for a in range(nx) for b in range(nz) if (a, b) != (0, 0)],
        key=lambda d: -ring_distance(d[0], nx) - ring_distance(d[1], nz),
    )
    y_devices = [device(d_y=d) for d in y_steps]
    plane_devices = [device(plane=d) for d in plane_steps]
    partner = device(other=True)
    corner_devices = [device(d_tm=a, d_y=b) for a in (1, -1) for b in (1, -1)]

    barrier = pltpu.get_barrier_semaphore()
    greeted = plane_devices + y_devices + corner_devices + [partner]
    for peer in greeted:
        pl.semaphore_signal(barrier, inc=1, device_id=peer, device_id_type=MESH)

    own_frames, own_rows = pl.ds(frames, frames), pl.ds(1, rows)
    lower = pl.multiple_of(s * lanes, lanes)
    loads = [
        pltpu.make_async_copy(features, x_ref.at[own_frames, own_rows], load_sem.at[0]),
        pltpu.make_async_copy(w_skip.at[pl.ds(lower, lanes)], ws, load_sem.at[1]),
        pltpu.make_async_copy(w_in.at[:, :, :, pl.ds(lower, lanes)], w1, load_sem.at[2]),
        pltpu.make_async_copy(w_mid, w2, load_sem.at[3]),
    ]
    vectors = [gain_in.at[pl.ds(lower, lanes)], shift_in.at[pl.ds(lower, lanes)], b_in, gain_mid, shift_mid, b_mid, b_skip]
    for i, vector in enumerate(vectors):
        loads.append(pltpu.make_async_copy(vector, small.at[i], load_sem.at[4 + i]))
    for load in loads:
        load.start()

    def local_stats(ref, width):
        def add(i, total):
            block = ref[frames + i // rows, 1 + lax.rem(i, rows)].astype(F32)
            return total + jnp.sum(block.reshape(cols // 8, 8, lanes), axis=0)

        total = lax.fori_loop(0, frames * rows, add, jnp.zeros((8, lanes), F32), unroll=4)
        total = jnp.sum(total, axis=0, keepdims=True)
        mean = lane_group_sum(jnp.broadcast_to(total, (8, lanes)), width) * (1.0 / (cells * width))

        def add_square(i, total):
            block = ref[frames + i // rows, 1 + lax.rem(i, rows)].astype(F32).reshape(cols // 8, 8, lanes)
            return total + jnp.sum(jnp.square(block - mean[None]), axis=0)

        spread = lax.fori_loop(0, frames * rows, add_square, jnp.zeros((8, lanes), F32), unroll=4)
        spread = jnp.sum(spread, axis=0, keepdims=True)
        spread = lane_group_sum(jnp.broadcast_to(spread, (8, lanes)), width)
        row = lax.broadcasted_iota(jnp.int32, (8, lanes), 0)
        return jnp.where(row == 0, mean, spread)

    def stat_phase(which, tile, devices, buffer):
        stat_out[which] = tile
        for j, peer in enumerate(devices):
            pltpu.make_async_remote_copy(
                src_ref=stat_out.at[which], dst_ref=buffer.at[which // 2, j],
                send_sem=stat_send.at[which], recv_sem=stat_recv.at[which],
                device_id=peer, device_id_type=MESH,
            ).start()

    def stat_wait(which, buffer):
        received = buffer.at[which // 2]
        pltpu.make_async_copy(received, received, stat_recv.at[which]).wait()
        return received[...]

    def stat_done(which, buffer):
        received = buffer.at[which // 2]
        pltpu.make_async_copy(received, received, stat_send.at[which]).wait()

    def halos(ref, at_cols, base):
        last = rows
        moves = [
            ((own_frames, own_rows), (pl.ds(0, frames), own_rows), device(d_tm=1)),
            ((own_frames, last), (own_frames, 0), device(d_y=1)),
            ((own_frames, 1), (own_frames, rows + 1), device(d_y=-1)),
            ((own_frames, last), (pl.ds(0, frames), 0), device(d_tm=1, d_y=1)),
            ((own_frames, 1), (pl.ds(0, frames), rows + 1), device(d_tm=1, d_y=-1)),
        ]
        return [
            pltpu.make_async_remote_copy(
                src_ref=ref.at[(*source, at_cols)], dst_ref=ref.at[(*target, at_cols)],
                send_sem=halo_send.at[base + i], recv_sem=halo_recv.at[base + i],
                device_id=peer, device_id_type=MESH,
            )
            for i, (source, target, peer) in enumerate(moves)
        ]

    def scales(tile, count, gain, shift):
        mean, spread = tile[0:1], tile[1:2] * (1.0 / count)
        scale = lax.rsqrt(spread + EPS) * small[gain:gain + 1, :]
        return mean, scale, small[shift:shift + 1, :]

    def activate(ref, at_cols, width, mean, scale, shift):
        place = lax.broadcasted_iota(jnp.int32, (width, lanes), 0)

        def one(i, carry):
            f, r = i // (rows + 2), lax.rem(i, rows + 2)
            from_f = jnp.where(tm == 0, jnp.maximum(f, frames), f)
            from_r = jnp.where(y == 0, jnp.maximum(r, 1), r)
            from_r = jnp.where(y == ny - 1, jnp.minimum(from_r, rows), from_r)
            block = ref[from_f, from_r, at_cols].astype(F32)
            block = silu((block - mean) * scale + shift)
            left = jnp.where(place == 0, block, pltpu.roll(block, 1, 0))
            right = jnp.where(place == width - 1, block, pltpu.roll(block, width - 1, 0))
            act[0, f, r, 0:width] = left.astype(BF16)
            act[1, f, r, 0:width] = block.astype(BF16)
            act[2, f, r, 0:width] = right.astype(BF16)
            return carry

        lax.fori_loop(0, 2 * frames * (rows + 2), one, 0, unroll=2)

    def convolve(weights, f, r, n_rows, at_cols, n_cols):
        taps = [(t, i, j) for t in range(3) for i in range(3) for j in range(3)]
        windows = [
            act[j, f + t, pl.ds(r + i, n_rows), at_cols].reshape(n_rows * n_cols, lanes) for t, i, j in taps
        ]
        total = jnp.zeros((n_rows * n_cols, lanes), F32)
        for k in range(0, len(taps), 2):
            window = jnp.concatenate(windows[k:k + 2], axis=1)
            matrix = jnp.concatenate([weights[tap] for tap in taps[k:k + 2]], axis=0)
            total = total + jnp.dot(window, matrix, preferred_element_type=F32)
        return total

    loads[0].wait()
    tile = local_stats(x_ref, 8)
    pl.semaphore_wait(barrier, len(greeted))
    stat_phase(0, tile, y_devices, y_buf)
    feature_halos = halos(x_ref, slice(None), 0)
    for copy in feature_halos:
        copy.start()

    loads[1].wait()
    their_cols, our_cols = pl.multiple_of((1 - s) * half, half), pl.multiple_of(s * half, half)

    def skip_product(start):
        block = x_ref[own_frames, own_rows, pl.ds(start, half)].reshape(frames * rows * half, lanes)
        return jnp.dot(block, ws[...], preferred_element_type=F32)

    skip_out[...] = skip_product(their_cols)
    skip_copy = pltpu.make_async_remote_copy(
        src_ref=skip_out, dst_ref=skip_in, send_sem=part_send.at[0], recv_sem=part_recv.at[0],
        device_id=partner, device_id_type=MESH,
    )
    skip_copy.start()
    skip_own[...] = skip_product(our_cols)
    for load in loads[2:]:
        load.wait()

    tile = combine(tile, stat_wait(0, y_buf), float(cells * 8))
    stat_phase(1, tile, plane_devices, xz_buf)
    tile = combine(tile, stat_wait(1, xz_buf), float(cells * 8 * ny))
    mean, scale, shift = scales(tile, float(cells * 8 * ny * ntm), 0, 1)
    for copy in feature_halos:
        copy.wait_recv()
    activate(x_ref, slice(None), cols, mean, scale, shift)

    pieces = part_own.shape[0]
    piece_rows = rows * frames // pieces

    def part_copy(i):
        return pltpu.make_async_remote_copy(
            src_ref=part_own.at[i], dst_ref=part_in.at[i],
            send_sem=part_send.at[1 + i], recv_sem=part_recv.at[1 + i],
            device_id=partner, device_id_type=MESH,
        )

    def first_piece(i, carry):
        f, r = (i * piece_rows) // rows, lax.rem(i * piece_rows, rows)
        part_own[i] = convolve(w1, f, r, piece_rows, slice(None), cols)
        part_copy(i).start()
        return carry

    lax.fori_loop(0, pieces, first_piece, 0)

    def hidden_piece(i, carry):
        f, r = (i * piece_rows) // rows, lax.rem(i * piece_rows, rows)
        part_copy(i).wait_recv()
        hidden = part_own[i] + part_in[i] + small[2:3, :]
        h_ref[frames + f, pl.ds(1 + r, piece_rows)] = hidden.astype(BF16).reshape(piece_rows, cols, lanes)
        return carry

    lax.fori_loop(0, pieces, hidden_piece, 0)

    tile = local_stats(h_ref, 4)
    stat_phase(2, tile, y_devices, y_buf)
    wide_start = pl.multiple_of(s * 16, 16)
    wide_cols = pl.ds(wide_start, wide)
    hidden_halos = halos(h_ref, wide_cols, len(feature_halos))
    for copy in hidden_halos:
        copy.start()
    skip_copy.wait_recv()
    skip_own[...] = skip_own[...] + skip_in[...] + (small[5:6, :] + small[6:7, :])
    tile = combine(tile, stat_wait(2, y_buf), float(cells * 4))
    stat_phase(3, tile, plane_devices, xz_buf)
    tile = combine(tile, stat_wait(3, xz_buf), float(cells * 4 * ny))
    mean, scale, shift = scales(tile, float(cells * 4 * ny * ntm), 3, 4)
    for copy in hidden_halos:
        copy.wait_recv()
    activate(h_ref, wide_cols, wide, mean, scale, shift)

    def second_piece(f, carry):
        size = rows * half
        total = convolve(w2, f, 0, rows, pl.ds(wide_start, half), half)
        total = total + skip_own[pl.ds(pl.multiple_of(f * size, size), size), :]
        out[f] = total.astype(BF16).reshape(rows, half, lanes)
        return carry

    lax.fori_loop(0, frames, second_piece, 0)

    for copy in feature_halos + hidden_halos + [skip_copy] + [part_copy(i) for i in range(pieces)]:
        copy.wait_send()
    for which, buffer in ((0, y_buf), (1, xz_buf), (2, y_buf), (3, xz_buf)):
        stat_done(which, buffer)


def shards(sizes, features, *others):
    nx, nz, ny = sizes
    frames, rows, cols, lanes = features.shape
    cells = frames * rows * cols
    pieces = 4
    dma = pltpu.SemaphoreType.DMA
    return pl.pallas_call(
        functools.partial(kernel, sizes),
        out_shape=jax.ShapeDtypeStruct((frames, rows, cols // 2, lanes), BF16),
        in_specs=[pl.BlockSpec(memory_space=pltpu.HBM)] * 11,
        out_specs=pl.BlockSpec(memory_space=pltpu.VMEM),
        scratch_shapes=[
            pltpu.VMEM((2 * frames, rows + 2, cols, lanes), BF16),
            pltpu.VMEM((2 * frames, rows + 2, cols, lanes), BF16),
            pltpu.VMEM((3, 2 * frames, rows + 2, cols, lanes), BF16),
            pltpu.VMEM((3, 3, 3, lanes, lanes), BF16),
            pltpu.VMEM((3, 3, 3, lanes, lanes), BF16),
            pltpu.VMEM((lanes, lanes), BF16),
            pltpu.VMEM((7, lanes), F32),
            pltpu.VMEM((pieces, cells // pieces, lanes), F32),
            pltpu.VMEM((pieces, cells // pieces, lanes), F32),
            pltpu.VMEM((cells // 2, lanes), F32),
            pltpu.VMEM((cells // 2, lanes), F32),
            pltpu.VMEM((cells // 2, lanes), F32),
            pltpu.VMEM((4, 8, lanes), F32),
            pltpu.VMEM((2, ny - 1, 8, lanes), F32),
            pltpu.VMEM((2, nx * nz - 1, 8, lanes), F32),
            dma((11,)), dma((4,)), dma((4,)), dma((10,)), dma((10,)), dma((pieces + 1,)), dma((pieces + 1,)),
        ],
        compiler_params=pltpu.CompilerParams(
            collective_id=0, has_side_effects=True, vmem_limit_bytes=40 * 2**20
        ),
        name="residual_block",
    )(*[pltpu.with_memory_space_constraint(array, pltpu.HBM) for array in (features, *others)])


def solution(mesh):
    nz = 8 if mesh.shape["tm"] % 8 == 0 else 2
    sizes = (mesh.shape["tm"] // nz, nz, mesh.shape["tile"])
    in_specs = (P("tm", "tile", None, "section"), P(), P(), P(), P(), P(), P(), P(), P(), P(), P())
    return jax.shard_map(
        functools.partial(shards, sizes), mesh=mesh, in_specs=in_specs,
        out_specs=P("tm", "tile", "section", None), check_vma=False,
    )
```

```python
import functools

import jax
import jax.numpy as jnp
from jax import lax
from jax.experimental import pallas as pl
from jax.experimental.pallas import tpu as pltpu
from jax.sharding import PartitionSpec as P

MESH = pl.DeviceIdType.MESH
EPS = 1e-06
F32 = jnp.float32
BF16 = jnp.bfloat16


def ring_distance(step, size):
    return min(step % size, (-step) % size)


def lane_group_sum(values, width):
    lanes = values.shape[-1]
    lane = lax.broadcasted_iota(jnp.int32, values.shape, values.ndim - 1)
    step = 1
    while step < width:
        upper = lax.rem(lane, 2 * step) >= step
        values = values + jnp.where(
            upper, pltpu.roll(values, step, 1), pltpu.roll(values, lanes - step, 1)
        )
        step *= 2
    return values


def combine(own, others, count):
    parts = others.shape[0] + 1
    total = own + jnp.sum(others, axis=0)
    mean = total * (1.0 / parts)
    spread = jnp.square(own - mean) + jnp.sum(jnp.square(others - mean[None]), axis=0)
    row = lax.broadcasted_iota(jnp.int32, own.shape, 0)
    return jnp.where(row == 0, mean, total + count * spread[0:1])


def silu(values):
    halved = 0.5 * values
    return halved + halved * jnp.tanh(halved)


def kernel(
    sizes,
    features, gain_in, shift_in, w_in, b_in, gain_mid, shift_mid, w_mid, b_mid, w_skip, b_skip,
    out,
    x_ref, h_ref, act, w1, w2, ws, small,
    part_own, part_in, skip_own, skip_out, skip_in,
    stat_out, y_buf, xz_buf,
    load_sem, stat_send, stat_recv, halo_send, halo_recv, part_send, part_recv,
):
    nx, nz, ny = sizes
    s, tm, y = lax.axis_index("section"), lax.axis_index("tm"), lax.axis_index("tile")
    ntm = nx * nz
    x, z = tm // nz, lax.rem(tm, nz)
    frames, rows, cols, lanes = features.shape
    half = cols // 2
    wide = half + 16
    cells = frames * rows * cols

    def device(d_tm=None, d_y=0, plane=None, other=False):
        new_tm = tm
        if d_tm is not None:
            new_tm = lax.rem(tm + d_tm + ntm, ntm)
        if plane is not None:
            new_tm = plane[0] * nz + lax.rem(z + plane[1], nz)
        new_y = lax.rem(y + d_y + ny, ny) if d_y else y
        return {"section": 1 - s if other else s, "tm": new_tm, "tile": new_y}

    near = x + 1 - 2 * lax.rem(x, 2)
    far = nx - 1 - x
    y_devices = [
        device(d_y=d, plane=(to_x, 0))
        for d, to_x in sorted(
            [(d, to_x) for d in range(ny) for to_x in (x, near) if d or to_x is near],
            key=lambda pair: -ring_distance(pair[0], ny),
        )
    ]
    plane_devices = [
        device(plane=(to_x, d))
        for d, to_x in sorted(
            [(d, to_x) for d in range(nz) for to_x in (x, far) if d or to_x is far],
            key=lambda pair: -ring_distance(pair[0], nz),
        )
    ]
    partner = device(other=True)
    corner_devices = [device(d_tm=a, d_y=b) for a in (1, -1) for b in (1, -1)]

    barrier = pltpu.get_barrier_semaphore()
    greeted = plane_devices + y_devices + corner_devices + [device(d_tm=1), device(d_tm=-1), partner]
    for peer in greeted:
        pl.semaphore_signal(barrier, inc=1, device_id=peer, device_id_type=MESH)

    own_frames, own_rows = pl.ds(frames, frames), pl.ds(1, rows)
    lower = pl.multiple_of(s * lanes, lanes)
    loads = [
        pltpu.make_async_copy(features, x_ref.at[own_frames, own_rows], load_sem.at[0]),
        pltpu.make_async_copy(w_skip.at[pl.ds(lower, lanes)], ws, load_sem.at[1]),
        pltpu.make_async_copy(w_in.at[:, :, :, pl.ds(lower, lanes)], w1, load_sem.at[2]),
        pltpu.make_async_copy(w_mid, w2, load_sem.at[3]),
    ]
    vectors = [gain_in.at[pl.ds(lower, lanes)], shift_in.at[pl.ds(lower, lanes)], b_in, gain_mid, shift_mid, b_mid, b_skip]
    for i, vector in enumerate(vectors):
        loads.append(pltpu.make_async_copy(vector, small.at[i], load_sem.at[4 + i]))
    for load in loads:
        load.start()

    def local_stats(ref, width):
        def add(i, total):
            block = ref[frames + i // rows, 1 + lax.rem(i, rows)].astype(F32)
            return total + jnp.sum(block.reshape(cols // 8, 8, lanes), axis=0)

        total = lax.fori_loop(0, frames * rows, add, jnp.zeros((8, lanes), F32), unroll=4)
        total = jnp.sum(total, axis=0, keepdims=True)
        mean = lane_group_sum(jnp.broadcast_to(total, (8, lanes)), width) * (1.0 / (cells * width))

        def add_square(i, total):
            block = ref[frames + i // rows, 1 + lax.rem(i, rows)].astype(F32).reshape(cols // 8, 8, lanes)
            return total + jnp.sum(jnp.square(block - mean[None]), axis=0)

        spread = lax.fori_loop(0, frames * rows, add_square, jnp.zeros((8, lanes), F32), unroll=4)
        spread = jnp.sum(spread, axis=0, keepdims=True)
        spread = lane_group_sum(jnp.broadcast_to(spread, (8, lanes)), width)
        row = lax.broadcasted_iota(jnp.int32, (8, lanes), 0)
        return jnp.where(row == 0, mean, spread)

    def stat_phase(which, tile, devices, buffer):
        stat_out[which] = tile
        for j, peer in enumerate(devices):
            pltpu.make_async_remote_copy(
                src_ref=stat_out.at[which], dst_ref=buffer.at[which // 2, j],
                send_sem=stat_send.at[which], recv_sem=stat_recv.at[which],
                device_id=peer, device_id_type=MESH,
            ).start()

    def stat_wait(which, buffer):
        received = buffer.at[which // 2]
        pltpu.make_async_copy(received, received, stat_recv.at[which]).wait()
        return received[...]

    def stat_done(which, buffer):
        received = buffer.at[which // 2]
        pltpu.make_async_copy(received, received, stat_send.at[which]).wait()

    def halos(ref, at_cols, base):
        last = rows
        moves = [
            ((own_frames, own_rows), (pl.ds(0, frames), own_rows), device(d_tm=1)),
            ((own_frames, last), (own_frames, 0), device(d_y=1)),
            ((own_frames, 1), (own_frames, rows + 1), device(d_y=-1)),
            ((own_frames, last), (pl.ds(0, frames), 0), device(d_tm=1, d_y=1)),
            ((own_frames, 1), (pl.ds(0, frames), rows + 1), device(d_tm=1, d_y=-1)),
        ]
        return [
            pltpu.make_async_remote_copy(
                src_ref=ref.at[(*source, at_cols)], dst_ref=ref.at[(*target, at_cols)],
                send_sem=halo_send.at[base + i], recv_sem=halo_recv.at[base + i],
                device_id=peer, device_id_type=MESH,
            )
            for i, (source, target, peer) in enumerate(moves)
        ]

    def scales(tile, count, gain, shift):
        mean, spread = tile[0:1], tile[1:2] * (1.0 / count)
        scale = lax.rsqrt(spread + EPS) * small[gain:gain + 1, :]
        return mean, scale, small[shift:shift + 1, :]

    def activate(ref, at_cols, width, mean, scale, shift):
        place = lax.broadcasted_iota(jnp.int32, (width, lanes), 0)

        def one(i, carry):
            f, r = i // (rows + 2), lax.rem(i, rows + 2)
            from_f = jnp.where(tm == 0, jnp.maximum(f, frames), f)
            from_r = jnp.where(y == 0, jnp.maximum(r, 1), r)
            from_r = jnp.where(y == ny - 1, jnp.minimum(from_r, rows), from_r)
            block = ref[from_f, from_r, at_cols].astype(F32)
            block = silu((block - mean) * scale + shift)
            left = jnp.where(place == 0, block, pltpu.roll(block, 1, 0))
            right = jnp.where(place == width - 1, block, pltpu.roll(block, width - 1, 0))
            act[0, f, r, 0:width] = left.astype(BF16)
            act[1, f, r, 0:width] = block.astype(BF16)
            act[2, f, r, 0:width] = right.astype(BF16)
            return carry

        lax.fori_loop(0, 2 * frames * (rows + 2), one, 0, unroll=2)

    def convolve(weights, f, r, n_rows, at_cols, n_cols):
        taps = [(t, i, j) for t in range(3) for i in range(3) for j in range(3)]
        windows = [
            act[j, f + t, pl.ds(r + i, n_rows), at_cols].reshape(n_rows * n_cols, lanes) for t, i, j in taps
        ]
        total = jnp.zeros((n_rows * n_cols, lanes), F32)
        for k in range(0, len(taps), 2):
            window = jnp.concatenate(windows[k:k + 2], axis=1)
            matrix = jnp.concatenate([weights[tap] for tap in taps[k:k + 2]], axis=0)
            total = total + jnp.dot(window, matrix, preferred_element_type=F32)
        return total

    loads[0].wait()
    tile = local_stats(x_ref, 8)
    pl.semaphore_wait(barrier, len(greeted))
    stat_phase(0, tile, y_devices, y_buf)
    feature_halos = halos(x_ref, slice(None), 0)
    for copy in feature_halos:
        copy.start()

    loads[1].wait()
    their_cols, our_cols = pl.multiple_of((1 - s) * half, half), pl.multiple_of(s * half, half)

    def skip_product(start):
        block = x_ref[own_frames, own_rows, pl.ds(start, half)].reshape(frames * rows * half, lanes)
        return jnp.dot(block, ws[...], preferred_element_type=F32)

    skip_out[...] = skip_product(their_cols)
    skip_copy = pltpu.make_async_remote_copy(
        src_ref=skip_out, dst_ref=skip_in, send_sem=part_send.at[0], recv_sem=part_recv.at[0],
        device_id=partner, device_id_type=MESH,
    )
    skip_copy.start()
    skip_own[...] = skip_product(our_cols)
    for load in loads[2:]:
        load.wait()

    tile = combine(tile, stat_wait(0, y_buf), float(cells * 8))
    stat_phase(1, tile, plane_devices, xz_buf)
    tile = combine(tile, stat_wait(1, xz_buf), float(cells * 8 * 2 * ny))
    mean, scale, shift = scales(tile, float(cells * 8 * ny * ntm), 0, 1)
    for copy in feature_halos:
        copy.wait_recv()
    activate(x_ref, slice(None), cols, mean, scale, shift)

    pieces = part_own.shape[0]
    piece_rows = rows * frames // pieces

    def part_copy(i):
        return pltpu.make_async_remote_copy(
            src_ref=part_own.at[i], dst_ref=part_in.at[i],
            send_sem=part_send.at[1 + i], recv_sem=part_recv.at[1 + i],
            device_id=partner, device_id_type=MESH,
        )

    def first_piece(i, carry):
        f, r = (i * piece_rows) // rows, lax.rem(i * piece_rows, rows)
        part_own[i] = convolve(w1, f, r, piece_rows, slice(None), cols)
        part_copy(i).start()
        return carry

    lax.fori_loop(0, pieces, first_piece, 0)

    def hidden_piece(i, carry):
        f, r = (i * piece_rows) // rows, lax.rem(i * piece_rows, rows)
        part_copy(i).wait_recv()
        hidden = part_own[i] + part_in[i] + small[2:3, :]
        h_ref[frames + f, pl.ds(1 + r, piece_rows)] = hidden.astype(BF16).reshape(piece_rows, cols, lanes)
        return carry

    lax.fori_loop(0, pieces, hidden_piece, 0)

    tile = local_stats(h_ref, 4)
    stat_phase(2, tile, y_devices, y_buf)
    wide_start = pl.multiple_of(s * 16, 16)
    wide_cols = pl.ds(wide_start, wide)
    hidden_halos = halos(h_ref, wide_cols, len(feature_halos))
    for copy in hidden_halos:
        copy.start()
    skip_copy.wait_recv()
    skip_own[...] = skip_own[...] + skip_in[...] + (small[5:6, :] + small[6:7, :])
    tile = combine(tile, stat_wait(2, y_buf), float(cells * 4))
    stat_phase(3, tile, plane_devices, xz_buf)
    tile = combine(tile, stat_wait(3, xz_buf), float(cells * 4 * 2 * ny))
    mean, scale, shift = scales(tile, float(cells * 4 * ny * ntm), 3, 4)
    for copy in hidden_halos:
        copy.wait_recv()
    activate(h_ref, wide_cols, wide, mean, scale, shift)

    def second_piece(f, carry):
        size = rows * half
        total = convolve(w2, f, 0, rows, pl.ds(wide_start, half), half)
        total = total + skip_own[pl.ds(pl.multiple_of(f * size, size), size), :]
        out[f] = total.astype(BF16).reshape(rows, half, lanes)
        return carry

    lax.fori_loop(0, frames, second_piece, 0)

    for copy in feature_halos + hidden_halos + [skip_copy] + [part_copy(i) for i in range(pieces)]:
        copy.wait_send()
    for which, buffer in ((0, y_buf), (1, xz_buf), (2, y_buf), (3, xz_buf)):
        stat_done(which, buffer)


def shards(sizes, features, *others):
    nx, nz, ny = sizes
    frames, rows, cols, lanes = features.shape
    cells = frames * rows * cols
    pieces = 4
    dma = pltpu.SemaphoreType.DMA
    return pl.pallas_call(
        functools.partial(kernel, sizes),
        out_shape=jax.ShapeDtypeStruct((frames, rows, cols // 2, lanes), BF16),
        in_specs=[pl.BlockSpec(memory_space=pltpu.HBM)] * 11,
        out_specs=pl.BlockSpec(memory_space=pltpu.VMEM),
        scratch_shapes=[
            pltpu.VMEM((2 * frames, rows + 2, cols, lanes), BF16),
            pltpu.VMEM((2 * frames, rows + 2, cols, lanes), BF16),
            pltpu.VMEM((3, 2 * frames, rows + 2, cols, lanes), BF16),
            pltpu.VMEM((3, 3, 3, lanes, lanes), BF16),
            pltpu.VMEM((3, 3, 3, lanes, lanes), BF16),
            pltpu.VMEM((lanes, lanes), BF16),
            pltpu.VMEM((7, lanes), F32),
            pltpu.VMEM((pieces, cells // pieces, lanes), F32),
            pltpu.VMEM((pieces, cells // pieces, lanes), F32),
            pltpu.VMEM((cells // 2, lanes), F32),
            pltpu.VMEM((cells // 2, lanes), F32),
            pltpu.VMEM((cells // 2, lanes), F32),
            pltpu.VMEM((4, 8, lanes), F32),
            pltpu.VMEM((2, 2 * ny - 1, 8, lanes), F32),
            pltpu.VMEM((2, 2 * nz - 1, 8, lanes), F32),
            dma((11,)), dma((4,)), dma((4,)), dma((10,)), dma((10,)), dma((pieces + 1,)), dma((pieces + 1,)),
        ],
        compiler_params=pltpu.CompilerParams(
            collective_id=0, has_side_effects=True, vmem_limit_bytes=40 * 2**20
        ),
        name="residual_block",
    )(*[pltpu.with_memory_space_constraint(array, pltpu.HBM) for array in (features, *others)])


def solution(mesh):
    nz = 8 if mesh.shape["tm"] % 8 == 0 else 2
    sizes = (mesh.shape["tm"] // nz, nz, mesh.shape["tile"])
    in_specs = (P("tm", "tile", None, "section"), P(), P(), P(), P(), P(), P(), P(), P(), P(), P())
    return jax.shard_map(
        functools.partial(shards, sizes), mesh=mesh, in_specs=in_specs,
        out_specs=P("tm", "tile", "section", None), check_vma=False,
    )
```

```python
import functools

import jax
import jax.numpy as jnp
from jax import lax
from jax.experimental import pallas as pl
from jax.experimental.pallas import tpu as pltpu
from jax.sharding import PartitionSpec as P

MESH = pl.DeviceIdType.MESH
EPS = 1e-06
F32 = jnp.float32
BF16 = jnp.bfloat16


def ring_distance(step, size):
    return min(step % size, (-step) % size)


def lane_group_sum(values, width):
    lanes = values.shape[-1]
    lane = lax.broadcasted_iota(jnp.int32, values.shape, values.ndim - 1)
    step = 1
    while step < width:
        upper = lax.rem(lane, 2 * step) >= step
        values = values + jnp.where(
            upper, pltpu.roll(values, step, 1), pltpu.roll(values, lanes - step, 1)
        )
        step *= 2
    return values


def combine(own, others, count):
    parts = others.shape[0] + 1
    total = own + jnp.sum(others, axis=0)
    mean = total * (1.0 / parts)
    spread = jnp.square(own - mean) + jnp.sum(jnp.square(others - mean[None]), axis=0)
    row = lax.broadcasted_iota(jnp.int32, own.shape, 0)
    return jnp.where(row == 0, mean, total + count * spread[0:1])


def silu(values):
    halved = 0.5 * values
    return halved + halved * jnp.tanh(halved)


def kernel(
    sizes,
    features, gain_in, shift_in, w_in, b_in, gain_mid, shift_mid, w_mid, b_mid, w_skip, b_skip,
    out,
    x_ref, h_ref, act, w1, w2, ws, small,
    part_own, part_in, skip_own, skip_out, skip_in,
    stat_out, y_buf, xz_buf,
    load_sem, stat_send, stat_recv, halo_send, halo_recv, part_send, part_recv,
):
    nx, nz, ny = sizes
    s, tm, y = lax.axis_index("section"), lax.axis_index("tm"), lax.axis_index("tile")
    ntm = nx * nz
    x, z = tm // nz, lax.rem(tm, nz)
    frames, rows, cols, lanes = features.shape
    half = cols // 2
    wide = half + 16
    cells = frames * rows * cols

    def device(d_tm=None, d_y=0, plane=None, other=False):
        new_tm = tm
        if d_tm is not None:
            new_tm = lax.rem(tm + d_tm + ntm, ntm)
        if plane is not None:
            new_tm = plane[0] * nz + lax.rem(z + plane[1], nz)
        new_y = lax.rem(y + d_y + ny, ny) if d_y else y
        return {"section": 1 - s if other else s, "tm": new_tm, "tile": new_y}

    near = x + 1 - 2 * lax.rem(x, 2)
    far = nx - 1 - x
    y_devices = [
        device(d_y=d, plane=(to_x, 0))
        for d, to_x in sorted(
            [(d, to_x) for d in range(ny) for to_x in (x, near) if d or to_x is near],
            key=lambda pair: -ring_distance(pair[0], ny),
        )
    ]
    plane_devices = [
        device(plane=(to_x, d))
        for d, to_x in sorted(
            [(d, to_x) for d in range(nz) for to_x in (x, far) if d or to_x is far],
            key=lambda pair: -ring_distance(pair[0], nz),
        )
    ]
    partner = device(other=True)
    corner_devices = [device(d_tm=a, d_y=b) for a in (1, -1) for b in (1, -1)]

    barrier = pltpu.get_barrier_semaphore()
    greeted = plane_devices + y_devices + corner_devices + [device(d_tm=1), device(d_tm=-1), partner]
    own_frames, own_rows = pl.ds(frames, frames), pl.ds(1, rows)
    lower = pl.multiple_of(s * lanes, lanes)
    loads = [
        pltpu.make_async_copy(features, x_ref.at[own_frames, own_rows], load_sem.at[0]),
        pltpu.make_async_copy(w_skip.at[pl.ds(lower, lanes)], ws, load_sem.at[1]),
        pltpu.make_async_copy(w_in.at[:, :, :, pl.ds(lower, lanes)], w1, load_sem.at[2]),
        pltpu.make_async_copy(w_mid, w2, load_sem.at[3]),
    ]
    vectors = [gain_in.at[pl.ds(lower, lanes)], shift_in.at[pl.ds(lower, lanes)], b_in, gain_mid, shift_mid, b_mid, b_skip]
    for i, vector in enumerate(vectors):
        loads.append(pltpu.make_async_copy(vector, small.at[i], load_sem.at[4 + i]))
    loads[0].start()
    for peer in greeted:
        pl.semaphore_signal(barrier, inc=1, device_id=peer, device_id_type=MESH)
    for load in loads[1:]:
        load.start()

    def local_stats(ref, width):
        def add(i, total):
            block = ref[frames + i // rows, 1 + lax.rem(i, rows)].astype(F32)
            return total + jnp.sum(block.reshape(cols // 8, 8, lanes), axis=0)

        total = lax.fori_loop(0, frames * rows, add, jnp.zeros((8, lanes), F32), unroll=16)
        total = jnp.sum(total, axis=0, keepdims=True)
        mean = lane_group_sum(jnp.broadcast_to(total, (8, lanes)), width) * (1.0 / (cells * width))

        def add_square(i, total):
            block = ref[frames + i // rows, 1 + lax.rem(i, rows)].astype(F32).reshape(cols // 8, 8, lanes)
            return total + jnp.sum(jnp.square(block - mean[None]), axis=0)

        spread = lax.fori_loop(0, frames * rows, add_square, jnp.zeros((8, lanes), F32), unroll=16)
        spread = jnp.sum(spread, axis=0, keepdims=True)
        spread = lane_group_sum(jnp.broadcast_to(spread, (8, lanes)), width)
        row = lax.broadcasted_iota(jnp.int32, (8, lanes), 0)
        return jnp.where(row == 0, mean, spread)

    def stat_phase(which, tile, devices, buffer):
        stat_out[which] = tile
        for j, peer in enumerate(devices):
            pltpu.make_async_remote_copy(
                src_ref=stat_out.at[which], dst_ref=buffer.at[which // 2, j],
                send_sem=stat_send.at[which], recv_sem=stat_recv.at[which],
                device_id=peer, device_id_type=MESH,
            ).start()

    def stat_wait(which, buffer):
        received = buffer.at[which // 2]
        pltpu.make_async_copy(received, received, stat_recv.at[which]).wait()
        return received[...]

    def stat_done(which, buffer):
        received = buffer.at[which // 2]
        pltpu.make_async_copy(received, received, stat_send.at[which]).wait()

    def halos(ref, at_cols, base):
        last = rows
        moves = [
            ((own_frames, own_rows), (pl.ds(0, frames), own_rows), device(d_tm=1)),
            ((own_frames, last), (own_frames, 0), device(d_y=1)),
            ((own_frames, 1), (own_frames, rows + 1), device(d_y=-1)),
            ((own_frames, last), (pl.ds(0, frames), 0), device(d_tm=1, d_y=1)),
            ((own_frames, 1), (pl.ds(0, frames), rows + 1), device(d_tm=1, d_y=-1)),
        ]
        return [
            pltpu.make_async_remote_copy(
                src_ref=ref.at[(*source, at_cols)], dst_ref=ref.at[(*target, at_cols)],
                send_sem=halo_send.at[base + i], recv_sem=halo_recv.at[base + i],
                device_id=peer, device_id_type=MESH,
            )
            for i, (source, target, peer) in enumerate(moves)
        ]

    def scales(tile, count, gain, shift):
        mean, spread = tile[0:1], tile[1:2] * (1.0 / count)
        scale = lax.rsqrt(spread + EPS) * small[gain:gain + 1, :]
        return mean, scale, small[shift:shift + 1, :]

    def activate(ref, at_cols, width, mean, scale, shift):
        place = lax.broadcasted_iota(jnp.int32, (width, lanes), 0)

        def one(i, carry):
            f, r = i // (rows + 2), lax.rem(i, rows + 2)
            from_f = jnp.where(tm == 0, jnp.maximum(f, frames), f)
            from_r = jnp.where(y == 0, jnp.maximum(r, 1), r)
            from_r = jnp.where(y == ny - 1, jnp.minimum(from_r, rows), from_r)
            block = ref[from_f, from_r, at_cols].astype(F32)
            block = silu((block - mean) * scale + shift)
            left = jnp.where(place == 0, block, pltpu.roll(block, 1, 0))
            right = jnp.where(place == width - 1, block, pltpu.roll(block, width - 1, 0))
            act[0, f, r, 0:width] = left.astype(BF16)
            act[1, f, r, 0:width] = block.astype(BF16)
            act[2, f, r, 0:width] = right.astype(BF16)
            return carry

        lax.fori_loop(0, 2 * frames * (rows + 2), one, 0, unroll=8)

    def convolve(weights, f, r, n_rows, at_cols, n_cols):
        taps = [(t, i, j) for t in range(3) for i in range(3) for j in range(3)]
        windows = [
            act[j, f + t, pl.ds(r + i, n_rows), at_cols].reshape(n_rows * n_cols, lanes) for t, i, j in taps
        ]
        total = jnp.zeros((n_rows * n_cols, lanes), F32)
        for k in range(0, len(taps), 2):
            window = jnp.concatenate(windows[k:k + 2], axis=1)
            matrix = jnp.concatenate([weights[tap] for tap in taps[k:k + 2]], axis=0)
            total = total + jnp.dot(window, matrix, preferred_element_type=F32)
        return total

    loads[0].wait()
    tile = local_stats(x_ref, 8)
    pl.semaphore_wait(barrier, len(greeted))
    stat_phase(0, tile, y_devices, y_buf)
    feature_halos = halos(x_ref, slice(None), 0)
    for copy in feature_halos:
        copy.start()

    loads[1].wait()
    their_cols, our_cols = pl.multiple_of((1 - s) * half, half), pl.multiple_of(s * half, half)

    def skip_product(start):
        block = x_ref[own_frames, own_rows, pl.ds(start, half)].reshape(frames * rows * half, lanes)
        return jnp.dot(block, ws[...], preferred_element_type=F32)

    skip_out[...] = skip_product(their_cols)
    skip_copy = pltpu.make_async_remote_copy(
        src_ref=skip_out, dst_ref=skip_in, send_sem=part_send.at[0], recv_sem=part_recv.at[0],
        device_id=partner, device_id_type=MESH,
    )
    skip_copy.start()
    skip_own[...] = skip_product(our_cols)
    for load in loads[2:]:
        load.wait()

    tile = combine(tile, stat_wait(0, y_buf), float(cells * 8))
    stat_phase(1, tile, plane_devices, xz_buf)
    tile = combine(tile, stat_wait(1, xz_buf), float(cells * 8 * 2 * ny))
    mean, scale, shift = scales(tile, float(cells * 8 * ny * ntm), 0, 1)
    for copy in feature_halos:
        copy.wait_recv()
    activate(x_ref, slice(None), cols, mean, scale, shift)

    pieces = part_own.shape[0]
    piece_rows = rows * frames // pieces

    def part_copy(i):
        return pltpu.make_async_remote_copy(
            src_ref=part_own.at[i], dst_ref=part_in.at[i],
            send_sem=part_send.at[1 + i], recv_sem=part_recv.at[1 + i],
            device_id=partner, device_id_type=MESH,
        )

    def first_piece(i, carry):
        f, r = (i * piece_rows) // rows, lax.rem(i * piece_rows, rows)
        part_own[i] = convolve(w1, f, r, piece_rows, slice(None), cols)
        part_copy(i).start()
        return carry

    lax.fori_loop(0, pieces, first_piece, 0)

    def hidden_piece(i, carry):
        f, r = (i * piece_rows) // rows, lax.rem(i * piece_rows, rows)
        part_copy(i).wait_recv()
        hidden = part_own[i] + part_in[i] + small[2:3, :]
        h_ref[frames + f, pl.ds(1 + r, piece_rows)] = hidden.astype(BF16).reshape(piece_rows, cols, lanes)
        return carry

    lax.fori_loop(0, pieces, hidden_piece, 0)

    tile = local_stats(h_ref, 4)
    stat_phase(2, tile, y_devices, y_buf)
    wide_start = pl.multiple_of(s * 16, 16)
    wide_cols = pl.ds(wide_start, wide)
    hidden_halos = halos(h_ref, wide_cols, len(feature_halos))
    for copy in hidden_halos:
        copy.start()
    skip_copy.wait_recv()
    skip_own[...] = skip_own[...] + skip_in[...] + (small[5:6, :] + small[6:7, :])
    tile = combine(tile, stat_wait(2, y_buf), float(cells * 4))
    stat_phase(3, tile, plane_devices, xz_buf)
    tile = combine(tile, stat_wait(3, xz_buf), float(cells * 4 * 2 * ny))
    mean, scale, shift = scales(tile, float(cells * 4 * ny * ntm), 3, 4)
    for copy in hidden_halos:
        copy.wait_recv()
    activate(h_ref, wide_cols, wide, mean, scale, shift)

    def second_piece(f, carry):
        size = rows * half
        total = convolve(w2, f, 0, rows, pl.ds(wide_start, half), half)
        total = total + skip_own[pl.ds(pl.multiple_of(f * size, size), size), :]
        out[f] = total.astype(BF16).reshape(rows, half, lanes)
        return carry

    lax.fori_loop(0, frames, second_piece, 0)

    for copy in feature_halos + hidden_halos + [skip_copy] + [part_copy(i) for i in range(pieces)]:
        copy.wait_send()
    for which, buffer in ((0, y_buf), (1, xz_buf), (2, y_buf), (3, xz_buf)):
        stat_done(which, buffer)


def shards(sizes, features, *others):
    nx, nz, ny = sizes
    frames, rows, cols, lanes = features.shape
    cells = frames * rows * cols
    pieces = 4
    dma = pltpu.SemaphoreType.DMA
    return pl.pallas_call(
        functools.partial(kernel, sizes),
        out_shape=jax.ShapeDtypeStruct((frames, rows, cols // 2, lanes), BF16),
        in_specs=[pl.BlockSpec(memory_space=pltpu.HBM)] * 11,
        out_specs=pl.BlockSpec(memory_space=pltpu.VMEM),
        scratch_shapes=[
            pltpu.VMEM((2 * frames, rows + 2, cols, lanes), BF16),
            pltpu.VMEM((2 * frames, rows + 2, cols, lanes), BF16),
            pltpu.VMEM((3, 2 * frames, rows + 2, cols, lanes), BF16),
            pltpu.VMEM((3, 3, 3, lanes, lanes), BF16),
            pltpu.VMEM((3, 3, 3, lanes, lanes), BF16),
            pltpu.VMEM((lanes, lanes), BF16),
            pltpu.VMEM((7, lanes), F32),
            pltpu.VMEM((pieces, cells // pieces, lanes), F32),
            pltpu.VMEM((pieces, cells // pieces, lanes), F32),
            pltpu.VMEM((cells // 2, lanes), F32),
            pltpu.VMEM((cells // 2, lanes), F32),
            pltpu.VMEM((cells // 2, lanes), F32),
            pltpu.VMEM((4, 8, lanes), F32),
            pltpu.VMEM((2, 2 * ny - 1, 8, lanes), F32),
            pltpu.VMEM((2, 2 * nz - 1, 8, lanes), F32),
            dma((11,)), dma((4,)), dma((4,)), dma((10,)), dma((10,)), dma((pieces + 1,)), dma((pieces + 1,)),
        ],
        compiler_params=pltpu.CompilerParams(
            collective_id=0, has_side_effects=True, vmem_limit_bytes=40 * 2**20
        ),
        name="residual_block",
    )(*[pltpu.with_memory_space_constraint(array, pltpu.HBM) for array in (features, *others)])


def solution(mesh):
    nz = 8 if mesh.shape["tm"] % 8 == 0 else 2
    sizes = (mesh.shape["tm"] // nz, nz, mesh.shape["tile"])
    in_specs = (P("tm", "tile", None, "section"), P(), P(), P(), P(), P(), P(), P(), P(), P(), P())
    return jax.shard_map(
        functools.partial(shards, sizes), mesh=mesh, in_specs=in_specs,
        out_specs=P("tm", "tile", "section", None), check_vma=False,
    )
```
